32 devices in a mesh: dp: 4 (over y, x), fsdp: 8 (over z, core).
Axes of the slice: x: 2, y: 2, z: 4, core: 2. Of those that a mesh axis runs over, the one named last changes fastest.
Arguments:
- block_input: float32 [6144, 960], P(('dp', 'fsdp')), may hold values from -6 to 6
- positions: int32 [6144], P(('dp', 'fsdp')), may hold values from 0 to 1151, as said below
- gain_attn: bfloat16 [2, 960], P(None, 'fsdp'), may hold values from 0.5 to 1.5
- w_query: bfloat16 [2, 960, 960], P(None, 'dp', 'fsdp'), may hold values from -0.1875 to 0.1875
- w_key: bfloat16 [2, 960, 320], P(None, 'dp', 'fsdp'), may hold values from -0.1875 to 0.1875
- w_value: bfloat16 [2, 960, 320], P(None, 'dp', 'fsdp'), may hold values from -0.1875 to 0.1875
- w_out: bfloat16 [2, 960, 960], P(None, 'dp', 'fsdp'), may hold values from -2 to 2
- gain_mlp: bfloat16 [2, 960], P(None, 'fsdp'), may hold values from 0.5 to 1.5
- w_gate: bfloat16 [2, 960, 2560], P(None, 'dp', 'fsdp'), may hold values from -0.1875 to 0.1875
- w_up: bfloat16 [2, 960, 2560], P(None, 'dp', 'fsdp'), may hold values from -0.1875 to 0.1875
- w_down: bfloat16 [2, 2560, 960], P(None, 'dp', 'fsdp'), may hold values from -0.125 to 0.125
- cotangent: float32 [6144, 960], P(('dp', 'fsdp')), may hold values from -6 to 6
Outputs:
- output: float32 [6144, 960], P(('dp', 'fsdp'))
- input_grad: float32 [6144, 960], P(('dp', 'fsdp'))
- grad_gain_attn: float32 [2, 960], P(None, 'fsdp')
- grad_w_query: float32 [2, 960, 960], P(None, 'dp', 'fsdp')
- grad_w_key: float32 [2, 960, 320], P(None, 'dp', 'fsdp')
- grad_w_value: float32 [2, 960, 320], P(None, 'dp', 'fsdp')
- grad_w_out: float32 [2, 960, 960], P(None, 'dp', 'fsdp')
- grad_gain_mlp: float32 [2, 960], P(None, 'fsdp')
- grad_w_gate: float32 [2, 960, 2560], P(None, 'dp', 'fsdp')
- grad_w_up: float32 [2, 960, 2560], P(None, 'dp', 'fsdp')
- grad_w_down: float32 [2, 2560, 960], P(None, 'dp', 'fsdp')
The draws below stay inside these ranges and needn't reach their ends.
Inputs may be any that keep to these rules, and one draw needn't show every extreme that they name: In each sequence of 1536 tokens the positions start at 0 and rise by one from token to token except where a new document starts at 0; a sequence holds four documents, one of exactly 1152 tokens.
All inputs are finite; a program needn't handle non-finite values.
Results may differ from the reference program's by a relative error of at most 0.028.
Values may be sent and summed in bfloat16 or wider, within the bound.
No kernel may reach another device: no remote copies, remote signals or barrier semaphores. Data moves between devices by JAX's collectives and lax.ppermute only.
A program may use at most 192 MiB of HBM per device.

```python
import math
import jax
import jax.numpy as jnp
from jax import lax

D = 960
QUERY_HEADS = 15
KEY_VALUE_HEADS = 5
HEAD_SIZE = 64
FF = 2560
LAYERS = 2
SEQUENCE_TOKENS = 1536
TOKENS = 6144
QW = 960
KW = 320


def document_positions(key):
    first, second, third = jax.random.split(key, 3)
    leading = jax.random.randint(first, (), 1, SEQUENCE_TOKENS // 8)
    following = jax.random.randint(second, (), 1, SEQUENCE_TOKENS // 8)
    remainder = SEQUENCE_TOKENS // 4 - leading - following
    big_slot = jax.random.randint(third, (), 0, 4)
    shorts = jnp.stack([leading, following, remainder]).astype(jnp.int32)
    orders = jnp.arange(4, dtype=jnp.int32)
    chosen = jnp.clip(orders - (orders > big_slot).astype(jnp.int32), 0, 2)
    lengths = jnp.where(orders == big_slot, 3 * SEQUENCE_TOKENS // 4, shorts[chosen]).astype(jnp.int32)
    doc_ends = jnp.cumsum(lengths).astype(jnp.int32)
    tokens_at = jnp.arange(SEQUENCE_TOKENS, dtype=jnp.int32)
    document = jnp.sum((tokens_at[:, None] >= doc_ends[None, :3]).astype(jnp.int32), axis=1)
    begins = (doc_ends - lengths).astype(jnp.int32)
    return (tokens_at - begins[document]).astype(jnp.int32)


def draw_positions(key, part):
    base = jax.random.fold_in(key, 11)
    sequence_batch = TOKENS // SEQUENCE_TOKENS
    seq_keys = jax.random.split(base, sequence_batch)
    return jax.vmap(document_positions)(seq_keys).reshape(-1).astype(jnp.int32)


def shard_levels(stream_key, shape, pieces, smallest, top_value):
    def one(dim, blocks):
        heights = jax.random.uniform(jax.random.fold_in(jax.random.fold_in(stream_key, 6), dim), (blocks,), jnp.float32, smallest / len(pieces), top_value / len(pieces))
        return jnp.repeat(jnp.exp(heights), shape[dim] // blocks).reshape((-1,) + (1,) * (len(shape) - dim - 1))

    level = one(*pieces[0])
    for cut in pieces[1:]:
        level = level * one(*cut)
    return level


def normal_values(key, shape, width, reach, pieces=(), kind=jnp.bfloat16):
    drawn = width * jax.random.normal(key, shape, jnp.float32)
    if pieces:
        drawn = drawn * shard_levels(key, shape, pieces, -0.22, 0.18)
    return jnp.clip(drawn, -reach, reach).astype(kind)


def setup_inputs(seed: int = 0) -> dict:
    streams_of = jax.random.split(jax.random.key(seed), 13)
    block_input = normal_values(streams_of[0], (TOKENS, D), 1.0, 6.0, ((0, 32),), jnp.float32)
    positions = draw_positions(jax.random.fold_in(streams_of[12], 71), 0)
    gain_attn = jnp.clip(1.0 + 0.1 * jax.random.normal(streams_of[2], (LAYERS, D), jnp.float32), 0.5, 1.5).astype(jnp.bfloat16)
    w_query = normal_values(streams_of[3], (LAYERS, D, QW), D ** -0.5, 0.1875, ((1, 4), (2, 8)))
    w_key = normal_values(streams_of[4], (LAYERS, D, KW), D ** -0.5, 0.1875, ((1, 4), (2, 8)))
    w_value = normal_values(streams_of[5], (LAYERS, D, KW), D ** -0.5, 0.1875, ((1, 4), (2, 8)))
    w_out = normal_values(streams_of[6], (LAYERS, QW, D), (max(1, QW * 16 // SEQUENCE_TOKENS)) ** -0.5, 2.0, ((1, 4), (2, 8)))
    gain_mlp = jnp.clip(1.0 + 0.1 * jax.random.normal(streams_of[7], (LAYERS, D), jnp.float32), 0.5, 1.5).astype(jnp.bfloat16)
    w_gate = normal_values(streams_of[8], (LAYERS, D, FF), D ** -0.5, 0.1875, ((1, 4), (2, 8)))
    w_up = normal_values(streams_of[9], (LAYERS, D, FF), D ** -0.5, 0.1875, ((1, 4), (2, 8)))
    w_down = normal_values(streams_of[10], (LAYERS, FF, D), FF ** -0.5, 0.125, ((1, 4), (2, 8)))
    cotangent = normal_values(streams_of[11], (TOKENS, D), 1.0, 6.0, ((0, 32),), jnp.float32)
    return {"block_input": block_input, "positions": positions, "gain_attn": gain_attn, "w_query": w_query, "w_key": w_key, "w_value": w_value, "w_out": w_out, "gain_mlp": gain_mlp, "w_gate": w_gate, "w_up": w_up, "w_down": w_down, "cotangent": cotangent}


EPS = 1e-05
HIGH = lax.Precision.HIGHEST

@jax.custom_vjp
def reduced_precision(v):
    return lax.optimization_barrier(v.astype(jnp.bfloat16)).astype(jnp.float32)

@jax.custom_vjp
def low_back(v):
    return v

def low_keep(v):
    return (reduced_precision(v), None)

def low_pass(kept, grad):
    return (grad,)

def back_keep(v):
    return (v, None)

def back_low(kept, grad):
    return (reduced_precision(grad),)
reduced_precision.defvjp(low_keep, low_pass)
low_back.defvjp(back_keep, back_low)

def matmul(left, right):
    return jnp.dot(left, right, precision=HIGH, preferred_element_type=jnp.float32)

def apply_rotary(value_rows, cosine_table, sine_table):
    half = value_rows.shape[-1] // 2
    first = value_rows[..., :half]
    second = value_rows[..., half:]
    return jnp.concatenate([first * cosine_table - second * sine_table, second * cosine_table + first * sine_table], axis=-1)

def normalize(value_rows, gain):
    return value_rows * lax.rsqrt(lax.optimization_barrier(jnp.mean(value_rows * value_rows, axis=-1, keepdims=True)) + EPS) * gain

def attend_over_sequence(operands):
    query_rows, key_rows, value_rows, document_start = operands
    block = math.gcd(SEQUENCE_TOKENS, 512)

    def one_block(number):
        query_block = lax.dynamic_slice_in_dim(query_rows, number * block, block, 0)
        start_block = lax.dynamic_slice_in_dim(document_start, number * block, block, 0)
        query_position = number * block + jnp.arange(block, dtype=jnp.int32)
        key_at = jnp.arange(SEQUENCE_TOKENS, dtype=jnp.int32)
        seen = (key_at[None, :] <= query_position[:, None]) & (key_at[None, :] >= start_block[:, None])
        attention_scores = jnp.einsum('qhgd,khd->hgqk', query_block, key_rows, precision=HIGH) * 0.125
        attention_scores = low_back(attention_scores)
        layer_weights = jnp.where(seen[None, None], jnp.exp(attention_scores), 0.0)
        total_sum = lax.optimization_barrier(jnp.sum(layer_weights, axis=-1))
        mixed_heads = jnp.einsum('hgqk,khd->qhgd', reduced_precision(layer_weights), value_rows, precision=HIGH)
        mixed_heads = low_back(mixed_heads)
        return mixed_heads / jnp.transpose(total_sum, (2, 0, 1))[..., None]
    layer_result = lax.map(jax.checkpoint(one_block), jnp.arange(SEQUENCE_TOKENS // block, dtype=jnp.int32))
    return layer_result.reshape(SEQUENCE_TOKENS, KEY_VALUE_HEADS, QUERY_HEADS // KEY_VALUE_HEADS, HEAD_SIZE)

def layer_forward(stream, document_start, cosine_table, sine_table, gain_a, wq, wk, wv, output_weight, gain_m, wg, wu, wd):
    token_count = stream.shape[0]
    hidden = reduced_precision(normalize(stream, gain_a))
    query_rows = low_back(matmul(hidden, wq))
    key_rows = low_back(matmul(hidden, wk))
    value_rows = low_back(matmul(hidden, wv))
    query_rows = reduced_precision(apply_rotary(query_rows.reshape(token_count, QUERY_HEADS, HEAD_SIZE), cosine_table[:, None], sine_table[:, None]))
    key_rows = reduced_precision(apply_rotary(key_rows.reshape(token_count, KEY_VALUE_HEADS, HEAD_SIZE), cosine_table[:, None], sine_table[:, None]))
    value_rows = reduced_precision(value_rows.reshape(token_count, KEY_VALUE_HEADS, HEAD_SIZE))
    sequence_batch = token_count // SEQUENCE_TOKENS
    mixed_heads = lax.map(attend_over_sequence, (query_rows.reshape(sequence_batch, SEQUENCE_TOKENS, KEY_VALUE_HEADS, QUERY_HEADS // KEY_VALUE_HEADS, HEAD_SIZE), key_rows.reshape(sequence_batch, SEQUENCE_TOKENS, KEY_VALUE_HEADS, HEAD_SIZE), value_rows.reshape(sequence_batch, SEQUENCE_TOKENS, KEY_VALUE_HEADS, HEAD_SIZE), document_start.reshape(sequence_batch, SEQUENCE_TOKENS)))
    mixed_heads = reduced_precision(mixed_heads.reshape(token_count, QUERY_HEADS * HEAD_SIZE))
    stream = stream + low_back(matmul(mixed_heads, output_weight))
    hidden = reduced_precision(normalize(stream, gain_m))
    gate = low_back(matmul(hidden, wg))
    upper = low_back(matmul(hidden, wu))
    active = reduced_precision(jax.nn.silu(gate) * upper)
    return stream + low_back(matmul(active, wd))

def reference(block_input, positions, gain_attn, w_query, w_key, w_value, w_out, gain_mlp, w_gate, w_up, w_down, cotangent):
    freq = 1.0 / jnp.power(10000.0, jnp.arange(0, HEAD_SIZE, 2).astype(jnp.float32) / HEAD_SIZE)
    angle = positions.astype(jnp.float32)[:, None] * freq[None, :]
    cosine_table = jnp.cos(angle)
    sine_table = jnp.sin(angle)
    document_start = (jnp.arange(positions.shape[0], dtype=jnp.int32) % SEQUENCE_TOKENS - positions).astype(jnp.int32)
    params = tuple((p.astype(jnp.float32) for p in (gain_attn, w_query, w_key, w_value, w_out, gain_mlp, w_gate, w_up, w_down)))

    def forward(stream, *layer_weights):
        for layer in range(LAYERS):
            stream = layer_forward(stream, document_start, cosine_table, sine_table, *[w[layer] for w in layer_weights])
        return stream
    output, pull = jax.vjp(forward, block_input, *params)
    grads = pull(cotangent)
    return (output, grads[0], grads[1], grads[2], grads[3], grads[4], grads[5], grads[6], grads[7], grads[8], grads[9])
```

```python
import jax
import jax.numpy as jnp
from jax import lax
from jax.sharding import Mesh
from jax.sharding import PartitionSpec as P

QUERY_HEADS = 15
KEY_VALUE_HEADS = 5
HEAD_SIZE = 64
GROUPS = QUERY_HEADS // KEY_VALUE_HEADS
KW = KEY_VALUE_HEADS * HEAD_SIZE
QW = QUERY_HEADS * HEAD_SIZE
EPS = 1e-05
PAD = 8
F32 = jnp.float32
BF16 = jnp.bfloat16


def apply_rotary(rows, cosine, sine):
    half = rows.shape[-1] // 2
    first, second = rows[..., :half], rows[..., half:]
    return jnp.concatenate([first * cosine - second * sine, second * cosine + first * sine], axis=-1)


def inverse_rotary(rows, cosine, sine):
    return apply_rotary(rows, cosine, -sine)


def nt(left, right):
    return lax.dot_general(left, right, (((1,), (1,)), ((), ())), preferred_element_type=F32)


def nn(left, right):
    return lax.dot_general(left, right, (((1,), (0,)), ((), ())), preferred_element_type=F32)


def tn(left, right):
    return lax.dot_general(left, right, (((0,), (0,)), ((), ())), preferred_element_type=F32)


def attention_forward(q, keys, values, query_at, doc_start):
    tokens, seq = q.shape[0], keys.shape[0]
    qh = q.reshape(tokens, KEY_VALUE_HEADS, GROUPS, HEAD_SIZE).transpose(1, 2, 0, 3)
    kh = keys.reshape(seq, KEY_VALUE_HEADS, HEAD_SIZE).transpose(1, 0, 2)
    vh = values.reshape(seq, KEY_VALUE_HEADS, HEAD_SIZE).transpose(1, 0, 2)
    key_at = jnp.arange(seq, dtype=jnp.int32)
    seen = (key_at[None] <= query_at[:, None]) & (key_at[None] >= doc_start[:, None])
    s = jnp.einsum("hgtd,hbd->hgtb", qh, kh, preferred_element_type=F32) * 0.125
    w = jnp.where(seen[None, None], jnp.exp(s), 0.0)
    total = jnp.sum(w, axis=-1)
    mixed = jnp.einsum("hgtb,hbd->hgtd", w.astype(BF16), vh, preferred_element_type=F32)
    head = mixed / total[..., None]
    return head.transpose(2, 0, 1, 3).reshape(tokens, QW), total


def attention_backward(q, keys, values, query_at, doc_start, head_out, total, grad_head):
    tokens, seq = q.shape[0], keys.shape[0]
    split = lambda v: v.reshape(tokens, KEY_VALUE_HEADS, GROUPS, HEAD_SIZE).transpose(1, 2, 0, 3)
    qh, ho, gh = split(q), split(head_out), split(grad_head)
    kh = keys.reshape(seq, KEY_VALUE_HEADS, HEAD_SIZE).transpose(1, 0, 2)
    vh = values.reshape(seq, KEY_VALUE_HEADS, HEAD_SIZE).transpose(1, 0, 2)
    grad_mixed = (gh / total[..., None]).astype(BF16)
    grad_total = -jnp.sum(gh * ho, axis=-1) / total
    key_at = jnp.arange(seq, dtype=jnp.int32)
    seen = (key_at[None] <= query_at[:, None]) & (key_at[None] >= doc_start[:, None])
    s = jnp.einsum("hgtd,hbd->hgtb", qh, kh, preferred_element_type=F32) * 0.125
    w = jnp.where(seen[None, None], jnp.exp(s), 0.0)
    back = jnp.einsum("hgtd,hbd->hgtb", grad_mixed, vh, preferred_element_type=F32)
    gs = (w * (back + grad_total[..., None])).astype(BF16)
    wl = w.astype(BF16)
    gq = 0.125 * jnp.einsum("hgtb,hbd->hgtd", gs, kh, preferred_element_type=F32)
    gk = 0.125 * jnp.einsum("hgtb,hgtd->hbd", gs, qh, preferred_element_type=F32)
    gv = jnp.einsum("hgtb,hgtd->hbd", wl, grad_mixed, preferred_element_type=F32)
    flat = lambda v: v.transpose(1, 0, 2).reshape(seq, KW)
    return gq.transpose(2, 0, 1, 3).reshape(tokens, QW), jnp.concatenate([flat(gk), flat(gv)], axis=1)


def make(mesh):
    nd, nf = mesh.shape["dp"], mesh.shape["fsdp"]
    nz = nf // 2
    per = nf // nd
    exchange = [(0, 1), (1, 0)]

    def to_peer(value, k):
        return lax.ppermute(value, "dp", [(i, i ^ k) for i in range(nd)])

    def on_device(block_input, positions, gain_attn, w_query, w_key, w_value, w_out, gain_mlp, w_gate, w_up, w_down, cotangent):
        layers, rows, qc = w_query.shape
        kc = w_key.shape[2]
        fc = w_gate.shape[2]
        sub = fc // nd
        tokens, width = block_input.shape
        local_ff = nf * sub
        chunk = 2 * qc + 2 * kc
        dp = lax.axis_index("dp")
        core = lax.axis_index("core")
        place = lax.axis_index("zz") * 2 + core
        relative = dp ^ jnp.arange(nd, dtype=jnp.int32)

        query_at = place * tokens + jnp.arange(tokens, dtype=jnp.int32)
        doc_start = query_at - positions
        freq = 1.0 / jnp.power(10000.0, jnp.arange(0, HEAD_SIZE, 2).astype(F32) / HEAD_SIZE)
        angle = positions.astype(F32)[:, None] * freq[None, :]
        cosine, sine = jnp.cos(angle)[:, None], jnp.sin(angle)[:, None]

        def by_block(value):
            return jnp.take(value.reshape(tokens, nd, rows).transpose(1, 0, 2), relative, axis=0)

        def from_block(parts):
            return jnp.take(jnp.stack(parts), relative, axis=0).transpose(1, 0, 2).reshape(tokens, width)

        def gather_attention(layer):
            gains = jnp.concatenate([gain_attn[layer], gain_mlp[layer]])[None]
            gains = jnp.pad(gains, ((0, PAD - 1), (0, 0)))
            mats = jnp.concatenate([w_query[layer], w_key[layer], w_value[layer], w_out[layer]], axis=1).T
            pack = jnp.concatenate([mats, gains], axis=0)
            half = lax.all_gather(pack, "zz", axis=0, tiled=False)
            mine = jnp.stack([half] + [to_peer(half, k) for k in range(1, nd)])
            other = lax.ppermute(mine, "core", exchange)
            full = jnp.where(core == 0, jnp.stack([mine, other], 2), jnp.stack([other, mine], 2))
            wq = full[:, :, :, :qc].reshape(nd, width, rows)
            wkv = jnp.concatenate(
                [full[:, :, :, qc : qc + kc].reshape(nd, KW, rows), full[:, :, :, qc + kc : qc + 2 * kc].reshape(nd, KW, rows)], axis=1
            )
            wo = full[:, :, :, qc + 2 * kc : chunk].reshape(nd, width, rows)
            row = full[0, :, :, chunk].astype(F32)
            return wq, wkv, wo, row[..., :qc].reshape(width), row[..., qc:].reshape(width)

        mlp_local = jnp.concatenate(
            [
                w_gate.reshape(layers, rows, nd, sub).transpose(2, 0, 3, 1),
                w_up.reshape(layers, rows, nd, sub).transpose(2, 0, 3, 1),
                w_down.reshape(layers, per, nd, sub, qc).transpose(2, 0, 3, 1, 4).reshape(nd, layers, sub, per * qc),
            ],
            axis=1,
        )
        attn = [gather_attention(0)]
        mlp_local = lax.all_to_all(mlp_local, "dp", 0, 0, tiled=True)

        def gather_mlp(layer):
            wg = mlp_local[:, layer].transpose(1, 0, 2).reshape(sub, width)
            wu = mlp_local[:, layers + layer].transpose(1, 0, 2).reshape(sub, width)
            wd = mlp_local[:, 2 * layers + layer].reshape(nd, sub, per, qc).transpose(3, 0, 2, 1).reshape(qc, local_ff)
            gu = lax.all_gather(jnp.concatenate([wg, wu], axis=0), ("zz", "core"), axis=0, tiled=True)
            gu = gu.reshape(nf, 2, sub, width).transpose(1, 0, 2, 3).reshape(2, local_ff, width)
            return gu[0], gu[1], lax.all_gather(wd, ("zz", "core"), axis=0, tiled=True)

        mlp = [gather_mlp(0)]
        for layer in range(1, layers):
            attn.append(gather_attention(layer))
            mlp.append(gather_mlp(layer))

        stream = block_input
        saved = []
        for layer in range(layers):
            wq, wkv, wo, gain_a, gain_m = attn[layer]
            wg, wu, wd = mlp[layer]
            inv1 = lax.rsqrt(jnp.mean(stream * stream, axis=-1, keepdims=True) + EPS)
            norm1 = stream * inv1
            hidden = by_block((norm1 * gain_a).astype(BF16))
            kv = sum(nt(hidden[k], wkv[k]) for k in range(nd))
            krot = apply_rotary(kv[:, :KW].reshape(tokens, KEY_VALUE_HEADS, HEAD_SIZE), cosine, sine).astype(BF16).reshape(tokens, KW)
            kv_all = lax.all_gather(jnp.concatenate([krot, kv[:, KW:].astype(BF16)], axis=1), ("zz", "core"), axis=0, tiled=True)
            q = sum(nt(hidden[k], wq[k]) for k in range(nd))
            qrot = apply_rotary(q.reshape(tokens, QUERY_HEADS, HEAD_SIZE), cosine, sine).astype(BF16).reshape(tokens, QW)
            head_out, total = attention_forward(qrot, kv_all[:, :KW], kv_all[:, KW:], query_at, doc_start)
            attn_low = by_block(head_out.astype(BF16))
            mid = stream + sum(nt(attn_low[k], wo[k]) for k in range(nd))
            inv2 = lax.rsqrt(jnp.mean(mid * mid, axis=-1, keepdims=True) + EPS)
            norm2 = mid * inv2
            h2 = (norm2 * gain_m).astype(BF16)
            hs = [h2] + [to_peer(h2, k) for k in range(1, nd)]
            gates, uppers, acts = [], [], []
            out = mid
            for k in range(nd):
                gate, upper = nt(hs[k], wg), nt(hs[k], wu)
                act = (jax.nn.silu(gate) * upper).astype(BF16)
                part = nt(act, wd)
                out = out + (part if k == 0 else to_peer(part.astype(BF16), k).astype(F32))
                gates.append(gate.astype(BF16))
                uppers.append(upper.astype(BF16))
                acts.append(act)
            saved.append((inv1, norm1, hidden, qrot, kv_all, head_out, total, attn_low, inv2, norm2, hs, gates, uppers, acts))
            stream = out

        grad = cotangent
        results = []
        for layer in reversed(range(layers)):
            inv1, norm1, hidden, qrot, kv_all, head_out, total, attn_low, inv2, norm2, hs, gates, uppers, acts = saved[layer]
            wq, wkv, wo, gain_a, gain_m = attn[layer]
            wg, wu, wd = mlp[layer]
            g_low = grad.astype(BF16)
            gs = [g_low] + [to_peer(g_low, k) for k in range(1, nd)]
            gh2 = None
            ggs, gus = [], []
            for k in range(nd):
                gate, upper = gates[k].astype(F32), uppers[k].astype(F32)
                gact = nn(gs[k], wd)
                sig = jax.nn.sigmoid(gate)
                gg = (gact * upper * sig * (1.0 + gate * (1.0 - sig))).astype(BF16)
                gu = (gact * gate * sig).astype(BF16)
                part = nn(gg, wg) + nn(gu, wu)
                gh2 = part if k == 0 else gh2 + to_peer(part.astype(BF16), k).astype(F32)
                ggs.append(gg)
                gus.append(gu)
            g_all, h_all = jnp.concatenate(gs, 0), jnp.concatenate(hs, 0)
            dwd = tn(g_all, jnp.concatenate(acts, 0)).astype(BF16)
            dwg = tn(jnp.concatenate(ggs, 0), h_all).astype(BF16)
            dwu = tn(jnp.concatenate(gus, 0), h_all).astype(BF16)
            dgu = jnp.stack([dwg.reshape(nf, sub, width), dwu.reshape(nf, sub, width)], 1).reshape(nf * 2 * sub, width)
            dgu = lax.psum_scatter(dgu, ("zz", "core"), scatter_dimension=0, tiled=True)
            dwd = lax.psum_scatter(dwd, ("zz", "core"), scatter_dimension=0, tiled=True)
            back = jnp.concatenate(
                [
                    dgu.reshape(2, sub, nd, rows).transpose(2, 0, 1, 3),
                    dwd.reshape(qc, nd, per, sub).transpose(1, 3, 2, 0).reshape(nd, 1, sub, per * qc),
                ],
                axis=1,
            )
            back = lax.all_to_all(back, "dp", 0, 0, tiled=True)
            grad_gate_w = back[:, 0].reshape(fc, rows).T.astype(F32)
            grad_up_w = back[:, 1].reshape(fc, rows).T.astype(F32)
            grad_down_w = back[:, 2].reshape(nd, sub, per, qc).transpose(2, 0, 1, 3).reshape(per * nd * sub, qc).astype(F32)

            grad_gain_m = jnp.sum(gh2 * norm2, axis=0)
            scaled = gh2 * gain_m
            gmid = grad + inv2 * (scaled - norm2 * jnp.mean(scaled * norm2, axis=-1, keepdims=True))
            ga = gmid.astype(BF16)
            grad_head = from_block([nn(ga, wo[k]) for k in range(nd)])
            gq, gkv = attention_backward(qrot, kv_all[:, :KW], kv_all[:, KW:], query_at, doc_start, head_out, total, grad_head)
            gkv = lax.psum_scatter(gkv.astype(BF16), ("zz", "core"), scatter_dimension=0, tiled=True).astype(F32)
            gq_low = inverse_rotary(gq.reshape(tokens, QUERY_HEADS, HEAD_SIZE), cosine, sine).reshape(tokens, QW).astype(BF16)
            gk_low = inverse_rotary(gkv[:, :KW].reshape(tokens, KEY_VALUE_HEADS, HEAD_SIZE), cosine, sine).reshape(tokens, KW).astype(BF16)
            gkv_low = jnp.concatenate([gk_low, gkv[:, KW:].astype(BF16)], axis=1)
            gh = from_block([nn(gq_low, wq[k]) + nn(gkv_low, wkv[k]) for k in range(nd)])
            grad_gain_a = jnp.sum(gh * norm1, axis=0)
            scaled = gh * gain_a
            grad = gmid + inv1 * (scaled - norm1 * jnp.mean(scaled * norm1, axis=-1, keepdims=True))

            gains = jnp.concatenate([grad_gain_a.reshape(nf, 1, qc), grad_gain_m.reshape(nf, 1, qc)], axis=2)
            gains = jnp.pad(gains, ((0, 0), (0, PAD - 1), (0, 0))).astype(BF16)
            packs = []
            for k in range(nd):
                dq = tn(gq_low, hidden[k]).astype(BF16).reshape(nf, qc, rows)
                dkv = tn(gkv_low, hidden[k]).astype(BF16).reshape(2, nf, kc, rows)
                do = tn(ga, attn_low[k]).astype(BF16).reshape(nf, qc, rows)
                packs.append(jnp.concatenate([dq, dkv[0], dkv[1], do, gains], axis=1))
            packs = jnp.stack(packs).reshape(nd, nz, 2, chunk + PAD, rows)
            keep = jnp.where(core == 0, packs[:, :, 0], packs[:, :, 1])
            send = jnp.where(core == 0, packs[:, :, 1], packs[:, :, 0])
            both = keep.astype(F32) + lax.ppermute(send, "core", exchange).astype(F32)
            low = both.astype(BF16)
            summed = both[0]
            for k in range(1, nd):
                summed = summed + to_peer(low[k], k).astype(F32)
            mine = lax.psum_scatter(summed.astype(BF16), "zz", scatter_dimension=0, tiled=False).astype(F32)
            results.append(
                (
                    mine[chunk, :qc],
                    mine[:qc].T,
                    mine[qc : qc + kc].T,
                    mine[qc + kc : qc + 2 * kc].T,
                    mine[qc + 2 * kc : chunk].T,
                    mine[chunk, qc:],
                    grad_gate_w,
                    grad_up_w,
                    grad_down_w,
                )
            )
        results = results[::-1]
        return (stream, grad) + tuple(jnp.stack([entry[n] for entry in results]) for n in range(9))

    return on_device


def solution(mesh):
    nd, nf = mesh.shape["dp"], mesh.shape["fsdp"]
    inner = Mesh(mesh.devices.reshape(nd, nf // 2, 2), ("dp", "zz", "core"))
    fs = ("zz", "core")
    rows = P(("dp", "zz", "core"), None)
    vector = P(None, fs)
    matrix = P(None, "dp", fs)
    in_specs = (rows, P(("dp", "zz", "core")), vector, matrix, matrix, matrix, matrix, vector, matrix, matrix, matrix, rows)
    out_specs = (rows, rows, vector, matrix, matrix, matrix, matrix, vector, matrix, matrix, matrix)
    return jax.shard_map(make(mesh), mesh=inner, in_specs=in_specs, out_specs=out_specs, check_vma=False)
```

```python
import jax
import jax.numpy as jnp
from jax import lax
from jax.experimental import pallas as pl
from jax.experimental.pallas import tpu as pltpu
from jax.sharding import Mesh
from jax.sharding import PartitionSpec as P

QUERY_HEADS = 15
KEY_VALUE_HEADS = 5
HEAD_SIZE = 64
GROUPS = QUERY_HEADS // KEY_VALUE_HEADS
KW = KEY_VALUE_HEADS * HEAD_SIZE
QW = QUERY_HEADS * HEAD_SIZE
EPS = 1e-05
KEY_BLOCK = 256
F32 = jnp.float32
BF16 = jnp.bfloat16


VM = pl.BlockSpec(memory_space=pltpu.VMEM)
SM = pl.BlockSpec(memory_space=pltpu.SMEM)
ANY = pl.BlockSpec(memory_space=pl.ANY)


def shaped(shape, dtype):
    return jax.ShapeDtypeStruct(shape, dtype)


def nt(left, right):
    return lax.dot_general(left, right, (((1,), (1,)), ((), ())), preferred_element_type=F32)


def nn(left, right):
    return lax.dot_general(left, right, (((1,), (0,)), ((), ())), preferred_element_type=F32)


def tn(left, right):
    return lax.dot_general(left, right, (((0,), (0,)), ((), ())), preferred_element_type=F32)


def swap_halves(x):
    half = HEAD_SIZE // 2
    return jnp.concatenate([x[:, half:], x[:, :half]], axis=1)


def inverse_rms(x):
    return lax.rsqrt(jnp.mean(x * x, axis=1, keepdims=True) + EPS)


def head(h):
    return slice(h * HEAD_SIZE, (h + 1) * HEAD_SIZE)


def round_up(n):
    return -(-n // 8) * 8


def assemble(blocks, place, nd, nz, sizes):
    offsets = [sum(sizes[:i]) for i in range(len(sizes))]

    def kernel(place_ref, *refs):
        ins, outs = refs[: 2 * nd], refs[2 * nd :]
        dp, zz, core = place_ref[0], place_ref[1], place_ref[2]
        for k in range(nd):
            j = dp ^ k
            for side in range(2):
                for z in range(nz):
                    f = (zz ^ z) * 2 + (core ^ side)
                    src = ins[side * nd + k]
                    outs[0][j, f] = src[z, offsets[0] : offsets[0] + sizes[0]]
                    outs[1][j, 0, f] = src[z, offsets[1] : offsets[1] + sizes[1]]
                    outs[1][j, 1, f] = src[z, offsets[2] : offsets[2] + sizes[2]]
                    outs[2][j, f] = src[z, offsets[3] : offsets[3] + sizes[3]]

    rows = blocks[0].shape[-1]
    nf = 2 * nz
    return pl.pallas_call(
        kernel,
        name="assemble",
        in_specs=[SM] + [VM] * (2 * nd),
        out_specs=[VM] * 3,
        out_shape=[
            shaped((nd, nf, sizes[0], rows), BF16),
            shaped((nd, 2, nf, sizes[1], rows), BF16),
            shaped((nd, nf, sizes[3], rows), BF16),
        ],
    )(place, *blocks)


def project_kv(parts, gain, wkv, cosine, sine):
    tokens, width = parts[0].shape
    nd, _, rows = wkv.shape
    n = len(parts)

    def kernel(*refs):
        ins = refs[:n]
        gain_ref, w_ref, cos_ref, sin_ref, stream_ref, h_ref, kv_ref = refs[n:]
        x = ins[0][...]
        for part in ins[1:]:
            x = x + part[...].astype(F32)
        stream_ref[...] = x
        h_ref[...] = (x * inverse_rms(x) * gain_ref[...]).astype(BF16)
        kv = nt(h_ref[:, :rows], w_ref[0])
        for j in range(1, nd):
            kv = kv + nt(h_ref[:, j * rows : (j + 1) * rows], w_ref[j])
        for g in range(KEY_VALUE_HEADS):
            k = kv[:, head(g)]
            kv_ref[:, head(g)] = (k * cos_ref[...] + swap_halves(k) * sin_ref[...]).astype(BF16)
        kv_ref[:, KW:] = kv[:, KW:].astype(BF16)

    return pl.pallas_call(
        kernel,
        name="project_kv",
        in_specs=[VM] * (n + 4),
        out_specs=[VM] * 3,
        out_shape=[shaped((tokens, width), F32), shaped((tokens, width), BF16), shaped((tokens, 2 * KW), BF16)],
    )(*parts, gain, wkv, cosine, sine)


def project_q(h, wq, cosine, sine):
    tokens = h.shape[0]
    nd, _, rows = wq.shape

    def kernel(h_ref, w_ref, cos_ref, sin_ref, qs_ref):
        q = nt(h_ref[:, :rows], w_ref[0])
        for j in range(1, nd):
            q = q + nt(h_ref[:, j * rows : (j + 1) * rows], w_ref[j])
        for i in range(QUERY_HEADS):
            x = q[:, head(i)]
            x = (x * cos_ref[...] + swap_halves(x) * sin_ref[...]).astype(BF16) * 0.125
            g, r = divmod(i, GROUPS)
            qs_ref[g, r * tokens : (r + 1) * tokens, :] = x.astype(BF16)

    return pl.pallas_call(
        kernel,
        name="project_q",
        in_specs=[VM] * 4,
        out_specs=VM,
        out_shape=shaped((KEY_VALUE_HEADS, GROUPS * tokens, HEAD_SIZE), BF16),
    )(h, wq, cosine, sine)


def attention_forward(scalars, qs, pieces, at, start, wo, stream, gain):
    tokens, width = stream.shape
    rows = GROUPS * tokens
    nd, _, part = wo.shape
    n = len(pieces)
    nz = n // 2

    def kernel(bounds_ref, qs_ref, *refs):
        ins = refs[:n]
        at_ref, start_ref, wo_ref, stream_ref, gain_ref, kv_ref, head_ref, inv_ref, low_ref, mid_ref, h2_ref, acc_ref, sum_ref = refs[n:]
        for side in range(2):
            for z in range(nz):
                f = (bounds_ref[2] ^ z) * 2 + (bounds_ref[3] ^ side)
                kv_ref[pl.ds(pl.multiple_of(f * tokens, tokens), tokens), :] = ins[side * nz + z][...]
        acc_ref[...] = jnp.zeros_like(acc_ref)
        sum_ref[...] = jnp.zeros_like(sum_ref)

        def step(block, carry):
            base = pl.multiple_of(block * KEY_BLOCK, KEY_BLOCK)
            key = base + lax.broadcasted_iota(jnp.int32, (tokens, KEY_BLOCK), 1)
            seen = (key <= at_ref[...]) & (key >= start_ref[...])
            bias = jnp.where(seen, 0.0, -1e30)
            bias = jnp.concatenate([bias] * GROUPS, axis=0)
            for g in range(KEY_VALUE_HEADS):
                k = kv_ref[pl.ds(base, KEY_BLOCK), head(g)]
                v = kv_ref[pl.ds(base, KEY_BLOCK), head(KEY_VALUE_HEADS + g)]
                w = jnp.exp(nt(qs_ref[g], k) + bias)
                piece = w[:, :128]
                for c in range(128, KEY_BLOCK, 128):
                    piece = piece + w[:, c : c + 128]
                sum_ref[g] += piece
                acc_ref[g] += nn(w.astype(BF16), v)
            return carry

        lax.fori_loop(bounds_ref[0], bounds_ref[1], step, 0)
        inv_ref[...] = jnp.zeros_like(inv_ref)
        for g in range(KEY_VALUE_HEADS):
            inv = 1.0 / jnp.sum(sum_ref[g], axis=1, keepdims=True)
            inv_ref[:, g : g + 1] = inv
            out = acc_ref[g] * inv
            for r in range(GROUPS):
                piece = out[r * tokens : (r + 1) * tokens]
                head_ref[:, head(g * GROUPS + r)] = piece
                low_ref[:, head(g * GROUPS + r)] = piece.astype(BF16)
        mid = stream_ref[...]
        for j in range(nd):
            mid = mid + nt(low_ref[:, j * part : (j + 1) * part], wo_ref[j])
        mid_ref[...] = mid
        h2_ref[...] = (mid * inverse_rms(mid) * gain_ref[...]).astype(BF16)

    return pl.pallas_call(
        kernel,
        name="attention_forward",
        in_specs=[SM] + [VM] * (6 + n),
        out_specs=[VM] * 6,
        out_shape=[
            shaped((n * tokens, 2 * KW), BF16),
            shaped((tokens, QW), F32),
            shaped((rows, 128), F32),
            shaped((tokens, QW), BF16),
            shaped((tokens, width), F32),
            shaped((tokens, width), BF16),
        ],
        scratch_shapes=[pltpu.VMEM((KEY_VALUE_HEADS, rows, HEAD_SIZE), F32), pltpu.VMEM((KEY_VALUE_HEADS, rows, 128), F32)],
    )(scalars, qs, *pieces, at, start, wo, stream, gain)


def attention_backward(scalars, grad, parts, mid, gain, wo, qs, kv, head_out, inv, cosine, sine, at, start):
    tokens, width = grad.shape
    rows = GROUPS * tokens
    nd, _, part = wo.shape
    n = len(parts)
    nz = kv.shape[0] // (2 * tokens)

    def kernel(bounds_ref, grad_ref, *refs):
        ins = refs[:n]
        mid_ref, gain_ref, wo_ref, qs_ref, kv_ref, ho_ref, inv_ref, cos_ref, sin_ref, at_ref, start_ref = refs[n : n + 11]
        gmid_ref, ga_ref, ggain_ref, gq_ref, keep_ref, send_ref, gkv_ref, gh_ref, gm_ref, gt_ref, acc_ref = refs[n + 11 :]
        gh2 = ins[0][...].astype(F32)
        for extra in ins[1:]:
            gh2 = gh2 + extra[...].astype(F32)
        mid = mid_ref[...]
        inverse = inverse_rms(mid)
        norm = mid * inverse
        weighted = gh2 * norm
        ggain_ref[...] = jnp.sum(weighted, axis=0, keepdims=True)
        mean = jnp.mean(weighted * gain_ref[...], axis=1, keepdims=True)
        gmid = grad_ref[...] + inverse * (gh2 * gain_ref[...] - norm * mean)
        gmid_ref[...] = gmid
        ga_ref[...] = gmid.astype(BF16)
        for j in range(nd):
            gh_ref[:, j * part : (j + 1) * part] = nn(ga_ref[...], wo_ref[j])
        gkv_ref[...] = jnp.zeros_like(gkv_ref)
        acc_ref[...] = jnp.zeros_like(acc_ref)
        for g in range(KEY_VALUE_HEADS):
            for r in range(GROUPS):
                here = slice(r * tokens, (r + 1) * tokens)
                scale = inv_ref[here, g : g + 1]
                gh = gh_ref[:, head(g * GROUPS + r)]
                gm_ref[g, here, :] = (gh * scale).astype(BF16)
                gt = -jnp.sum(gh * ho_ref[:, head(g * GROUPS + r)], axis=1, keepdims=True) * scale
                gt_ref[g : g + 1, here] = gt.T

        def step(block, carry):
            base = pl.multiple_of(block * KEY_BLOCK, KEY_BLOCK)
            key = base + lax.broadcasted_iota(jnp.int32, (KEY_BLOCK, rows), 0)
            seen = (key <= at_ref[...]) & (key >= start_ref[...])
            bias = jnp.where(seen, 0.0, -1e30)
            for g in range(KEY_VALUE_HEADS):
                k = kv_ref[pl.ds(base, KEY_BLOCK), head(g)]
                v = kv_ref[pl.ds(base, KEY_BLOCK), head(KEY_VALUE_HEADS + g)]
                w = jnp.exp(nt(k, qs_ref[g]) + bias)
                gs = (w * (nt(v, gm_ref[g]) + gt_ref[g : g + 1, :])).astype(BF16)
                gkv_ref[pl.ds(base, KEY_BLOCK), head(g)] = nn(gs, qs_ref[g]).astype(BF16)
                gkv_ref[pl.ds(base, KEY_BLOCK), head(KEY_VALUE_HEADS + g)] = nn(w.astype(BF16), gm_ref[g]).astype(BF16)
                acc_ref[g] += tn(gs, k)
            return carry

        lax.fori_loop(bounds_ref[0], bounds_ref[1], step, 0)
        for i in range(QUERY_HEADS):
            g, r = divmod(i, GROUPS)
            x = acc_ref[g, r * tokens : (r + 1) * tokens, :] * 0.125
            gq_ref[:, head(i)] = (x * cos_ref[...] - swap_halves(x) * sin_ref[...]).astype(BF16)
        for z in range(nz):
            for side, target in ((0, keep_ref), (1, send_ref)):
                f = (bounds_ref[2] ^ z) * 2 + (bounds_ref[3] ^ side)
                target[z] = gkv_ref[pl.ds(pl.multiple_of(f * tokens, tokens), tokens), :]

    return pl.pallas_call(
        kernel,
        name="attention_backward",
        in_specs=[SM] + [VM] * (n + 12),
        out_specs=[VM] * 6,
        out_shape=[
            shaped((tokens, width), F32),
            shaped((tokens, width), BF16),
            shaped((1, width), F32),
            shaped((tokens, QW), BF16),
            shaped((nz, tokens, 2 * KW), BF16),
            shaped((nz, tokens, 2 * KW), BF16),
        ],
        scratch_shapes=[
            pltpu.VMEM(kv.shape, BF16),
            pltpu.VMEM((tokens, QW), F32),
            pltpu.VMEM((KEY_VALUE_HEADS, rows, HEAD_SIZE), BF16),
            pltpu.VMEM((8, rows), F32),
            pltpu.VMEM((KEY_VALUE_HEADS, rows, HEAD_SIZE), F32),
        ],
    )(scalars, grad, *parts, mid, gain, wo, qs, kv, head_out, inv, cosine, sine, at, start)


def hidden_backward(gmid, stream, gain, gkvs, gq, wq, wkv, cosine, sine):
    tokens, width = gmid.shape
    nd, _, part = wq.shape
    n = len(gkvs)

    def kernel(gmid_ref, stream_ref, gain_ref, *refs):
        ins = refs[:n]
        gq_ref, wq_ref, wkv_ref, cos_ref, sin_ref, grad_ref, low_ref, gkl_ref, ggain_ref, gh_ref = refs[n:]
        total = ins[0][...].astype(F32)
        for piece in ins[1:]:
            total = total + piece[...].astype(F32)
        for g in range(KEY_VALUE_HEADS):
            k = total[:, head(g)]
            gkl_ref[:, head(g)] = (k * cos_ref[...] - swap_halves(k) * sin_ref[...]).astype(BF16)
        gkl_ref[:, KW:] = total[:, KW:].astype(BF16)
        for j in range(nd):
            gh_ref[:, j * part : (j + 1) * part] = nn(gq_ref[...], wq_ref[j]) + nn(gkl_ref[...], wkv_ref[j])
        gh = gh_ref[...]
        x = stream_ref[...]
        inverse = inverse_rms(x)
        norm = x * inverse
        weighted = gh * norm
        ggain_ref[...] = jnp.sum(weighted, axis=0, keepdims=True)
        mean = jnp.mean(weighted * gain_ref[...], axis=1, keepdims=True)
        grad = gmid_ref[...] + inverse * (gh * gain_ref[...] - norm * mean)
        grad_ref[...] = grad
        low_ref[...] = grad.astype(BF16)

    return pl.pallas_call(
        kernel,
        name="hidden_backward",
        in_specs=[VM] * (8 + n),
        out_specs=[VM] * 4,
        out_shape=[
            shaped((tokens, width), F32),
            shaped((tokens, width), BF16),
            shaped((tokens, 2 * KW), BF16),
            shaped((1, width), F32),
        ],
        scratch_shapes=[pltpu.VMEM((tokens, width), F32)],
    )(gmid, stream, gain, *gkvs, gq, wq, wkv, cosine, sine)


def attention_weight_grads(place, pairs, extra, nd, nz, counts):
    part = pairs[0][1].shape[1] // nd
    nf = 2 * nz
    flat_counts = [c for group in counts for c in group]
    sizes = [round_up(c) for c in flat_counts]
    offsets = [sum(sizes[:i]) for i in range(len(sizes) + 1)]
    total = offsets[-1] + (0 if extra is None else 8)
    operands = [v for pair in pairs for v in pair] + ([] if extra is None else [extra])
    tall = max(pair[0].shape[1] for pair in pairs)

    def kernel(place_ref, *refs):
        dp, zz, core = place_ref[0], place_ref[1], place_ref[2]
        ins, (keep_ref, send_ref, t_ref) = refs[: len(operands)], refs[len(operands) :]

        def put(z, j, offset, first, second):
            at = slice(offset, offset + first.shape[0])

            @pl.when(core == 0)
            def _():
                keep_ref[dp ^ j, zz ^ z, at, :] = first
                send_ref[dp ^ j, zz ^ z, at, :] = second

            @pl.when(core == 1)
            def _():
                keep_ref[dp ^ j, zz ^ z, at, :] = second
                send_ref[dp ^ j, zz ^ z, at, :] = first

        if sizes != flat_counts:
            keep_ref[...] = jnp.zeros_like(keep_ref)
            send_ref[...] = jnp.zeros_like(send_ref)
        for j in range(nd):
            m = 0
            for p in range(len(pairs)):
                t_ref[: pairs[p][0].shape[1], :] = tn(ins[2 * p][...], ins[2 * p + 1][:, j * part : (j + 1) * part]).astype(BF16)
                base = 0
                for count in counts[p]:
                    for z in range(nz):
                        low = base + 2 * z * count
                        put(z, j, offsets[m], t_ref[low : low + count, :], t_ref[low + count : low + 2 * count, :])
                    base += nf * count
                    m += 1
            if extra is not None:
                for z in range(nz):
                    put(z, j, offsets[m], ins[-1][2 * z], ins[-1][2 * z + 1])

    return pl.pallas_call(
        kernel,
        name="attention_weight_grads",
        in_specs=[SM] + [VM] * len(operands),
        out_specs=[VM] * 2,
        out_shape=[shaped((nd, nz, total, part), BF16)] * 2,
        scratch_shapes=[pltpu.VMEM((tall, part), BF16)],
    )(place, *operands)


def mlp_forward(hs, wg, wu, wd, own):
    tokens, width = hs[0].shape
    local = wg.shape[0]
    n = len(hs)

    def kernel(*refs):
        ins, (wg_ref, wu_ref, wd_ref), outs = refs[:n], refs[n : n + 3], refs[n + 3 :]
        for i in range(n):
            gate_ref, up_ref, act_ref, part_ref = outs[4 * i : 4 * i + 4]
            gate, up = nt(ins[i][...], wg_ref[...]), nt(ins[i][...], wu_ref[...])
            gate_ref[...] = gate.astype(BF16)
            up_ref[...] = up.astype(BF16)
            act_ref[...] = (gate * jax.nn.sigmoid(gate) * up).astype(BF16)
            part_ref[...] = nt(act_ref[...], wd_ref[...]).astype(part_ref.dtype)

    one = [shaped((tokens, local), BF16)] * 3 + [shaped((tokens, width), F32 if own else BF16)]
    flat = pl.pallas_call(kernel, name="mlp_forward", in_specs=[VM] * (n + 3), out_specs=[VM] * (4 * n), out_shape=one * n)(*hs, wg, wu, wd)
    return [flat[4 * i : 4 * i + 4] for i in range(n)]


def mlp_backward(gs, gates, ups, wg, wu, wd, own):
    tokens, width = gs[0].shape
    local = wg.shape[0]
    n = len(gs)

    def kernel(*refs):
        ins, (wg_ref, wu_ref, wd_ref), outs = refs[: 3 * n], refs[3 * n : 3 * n + 3], refs[3 * n + 3 :]
        for i in range(n):
            gg_ref, gu_ref, part_ref = outs[3 * i : 3 * i + 3]
            gact = nn(ins[i][...], wd_ref[...])
            gate, up = ins[n + i][...].astype(F32), ins[2 * n + i][...].astype(F32)
            sig = jax.nn.sigmoid(gate)
            gg_ref[...] = (gact * up * sig * (1.0 + gate * (1.0 - sig))).astype(BF16)
            gu_ref[...] = (gact * gate * sig).astype(BF16)
            part = nn(gg_ref[...], wg_ref[...]) + nn(gu_ref[...], wu_ref[...])
            part_ref[...] = part.astype(part_ref.dtype)

    one = [shaped((tokens, local), BF16)] * 2 + [shaped((tokens, width), F32 if own else BF16)]
    flat = pl.pallas_call(kernel, name="mlp_backward", in_specs=[VM] * (3 * n + 3), out_specs=[VM] * (3 * n), out_shape=one * n)(
        *gs, *gates, *ups, wg, wu, wd
    )
    return [flat[3 * i : 3 * i + 3] for i in range(n)]


def mlp_weight_grads(place, gs, acts, ggs, gus, hs, nz):
    n = len(gs)
    tokens, width = gs[0].shape
    local = acts[0].shape[1]
    nf = 2 * nz
    sub, qc = local // nf, width // nf

    def kernel(place_ref, *refs):
        zz, core = place_ref[1], place_ref[2]
        groups = [refs[i * n : (i + 1) * n] for i in range(5)]
        keep_ref, send_ref, dkeep_ref, dsend_ref, wide_ref, left_ref, out_ref, down_ref = refs[5 * n :]

        def fill(target, parts):
            for i in range(n):
                target[i * tokens : (i + 1) * tokens, :] = parts[i][...]

        fill(wide_ref, groups[4])
        for m in range(2):
            fill(left_ref, groups[2 + m])
            out_ref[...] = tn(left_ref[...], wide_ref[...]).astype(BF16).reshape(nf, sub, width)
            for z in range(nz):
                f = (zz ^ z) * 2 + core
                keep_ref[z, m * sub : (m + 1) * sub, :] = out_ref[f]
                send_ref[z, m * sub : (m + 1) * sub, :] = out_ref[f ^ 1]
        fill(wide_ref, groups[0])
        fill(left_ref, groups[1])
        down_ref[...] = tn(wide_ref[...], left_ref[...]).astype(BF16).reshape(nf, qc, local)
        for z in range(nz):
            f = (zz ^ z) * 2 + core
            dkeep_ref[z] = down_ref[f]
            dsend_ref[z] = down_ref[f ^ 1]

    return pl.pallas_call(
        kernel,
        name="mlp_weight_grads",
        in_specs=[SM] + [VM] * (5 * n),
        out_specs=[VM] * 4,
        out_shape=[shaped((nz, 2 * sub, width), BF16)] * 2 + [shaped((nz, qc, local), BF16)] * 2,
        scratch_shapes=[
            pltpu.VMEM((n * tokens, width), BF16),
            pltpu.VMEM((n * tokens, local), BF16),
            pltpu.VMEM((nf, sub, width), BF16),
            pltpu.VMEM((nf, qc, local), BF16),
        ],
    )(place, *gs, *acts, *ggs, *gus, *hs)


def make(mesh):
    nd, nf = mesh.shape["dp"], mesh.shape["fsdp"]
    nz = nf // 2
    per = nf // nd
    exchange = [(0, 1), (1, 0)]
    batches = [[0], [1, 2], list(range(3, nd))]
    fs = ("zz", "core")

    def to_peer(value, k):
        return lax.ppermute(value, "dp", [(i, i ^ k) for i in range(nd)])

    def to_z(value, k):
        return lax.ppermute(value, "zz", [(i, i ^ k) for i in range(nz)])

    def to_core(value):
        return lax.ppermute(value, "core", exchange)

    def on_device(block_input, positions, gain_attn, w_query, w_key, w_value, w_out, gain_mlp, w_gate, w_up, w_down, cotangent):
        layers, rows, qc = w_query.shape
        kc = w_key.shape[2]
        fc = w_gate.shape[2]
        sub = fc // nd
        tokens, width = block_input.shape
        local_ff = nf * sub
        counts = [qc, kc, kc, qc]
        sizes = [round_up(n) for n in counts]
        offsets = [sum(sizes[:i]) for i in range(5)]
        dp, zz, core = lax.axis_index("dp"), lax.axis_index("zz"), lax.axis_index("core")
        place = jnp.stack([dp, zz, core]).astype(jnp.int32)
        index = zz * 2 + core

        query_at = index * tokens + jnp.arange(tokens, dtype=jnp.int32)
        doc_start = query_at - positions
        freq = 1.0 / jnp.power(10000.0, jnp.arange(0, HEAD_SIZE, 2).astype(F32) / HEAD_SIZE)
        angle = positions.astype(F32)[:, None] * freq[None, :]
        cosine = jnp.concatenate([jnp.cos(angle)] * 2, axis=1)
        sine = jnp.concatenate([-jnp.sin(angle), jnp.sin(angle)], axis=1)
        bounds = jnp.stack([doc_start[0] // KEY_BLOCK, query_at[-1] // KEY_BLOCK + 1, zz, core]).astype(jnp.int32)
        columns = query_at[:, None], doc_start[:, None]
        lanes = jnp.tile(query_at, GROUPS)[None], jnp.tile(doc_start, GROUPS)[None]

        def pack_attention(layer):
            gains = jnp.concatenate([gain_attn[layer], gain_mlp[layer]])[None]
            mats = [w_query[layer].T, w_key[layer].T, w_value[layer].T, w_out[layer].T, gains]
            return jnp.concatenate([jnp.pad(m, ((0, round_up(m.shape[0]) - m.shape[0]), (0, 0))) for m in mats], axis=0)

        def gather_attention(layer, after=None):
            pack = pack_attention(layer)
            if after is not None:
                pack, _ = lax.optimization_barrier((pack, after))
            half = jnp.stack([pack] + [to_z(pack, k) for k in range(1, nz)])
            mine = [half] + [to_peer(half, k) for k in range(1, nd)]
            other = [to_core(m) for m in mine]
            return mine, other

        def use_attention(blocks):
            mine, other = blocks
            wq, wkv, wo = assemble(mine + other, place, nd, nz, sizes)
            pair = jnp.stack([mine[0][:, offsets[4]], other[0][:, offsets[4]]], 1)
            pair = jnp.where(core == 0, pair, pair[:, ::-1])
            row = jnp.take(pair, zz ^ jnp.arange(nz), axis=0).astype(F32)
            return (
                wq[:, :, :qc].reshape(nd, width, rows),
                wkv[:, :, :, :kc].reshape(nd, 2 * KW, rows),
                wo[:, :, :qc].reshape(nd, width, rows),
                row[..., :qc].reshape(1, width),
                row[..., qc:].reshape(1, width),
            )

        mlp_local = jnp.concatenate(
            [
                w_gate.reshape(layers, rows, nd, sub).transpose(2, 0, 3, 1),
                w_up.reshape(layers, rows, nd, sub).transpose(2, 0, 3, 1),
                w_down.reshape(layers, per, nd, sub, qc).transpose(2, 0, 3, 1, 4).reshape(nd, layers, sub, per * qc),
            ],
            axis=1,
        )
        pieces = [lax.dynamic_index_in_dim(mlp_local, dp ^ k, 0, keepdims=False) for k in range(nd)]
        pieces = [pieces[0]] + [to_peer(pieces[k], k) for k in range(1, nd)]
        mlp_local = jnp.take(jnp.stack(pieces), dp ^ jnp.arange(nd), axis=0)

        def gather_mlp(layer):
            wg = mlp_local[:, layer].transpose(1, 0, 2).reshape(sub, width)
            wu = mlp_local[:, layers + layer].transpose(1, 0, 2).reshape(sub, width)
            wd = mlp_local[:, 2 * layers + layer].reshape(nd, sub, per, qc).transpose(3, 0, 2, 1).reshape(qc, local_ff)
            gu = lax.all_gather(jnp.concatenate([wg, wu], axis=0), fs, axis=0, tiled=True)
            gu = gu.reshape(nf, 2, sub, width).transpose(1, 0, 2, 3).reshape(2, local_ff, width)
            return gu[0], gu[1], lax.all_gather(wd, fs, axis=0, tiled=True)

        attn = [use_attention(gather_attention(0))]
        mlp = [gather_mlp(layer) for layer in range(layers)]

        parts = [block_input]
        saved = []
        for layer in range(layers):
            wq, wkv, wo, gain_a, gain_m = attn[layer]
            wg, wu, wd = mlp[layer]
            stream, h, kv = project_kv(parts, gain_a, wkv, cosine, sine)
            near = [kv] + [to_z(kv, k) for k in range(1, nz)]
            kvs = near + [to_core(piece) for piece in near]
            qs = project_q(h, wq, cosine, sine)
            if layer + 1 < layers:
                pending = gather_attention(layer + 1, qs)
            kv_all, head_out, inv, low, mid, h2 = attention_forward(bounds, qs, kvs, *columns, wo, stream, gain_m)
            hs = [h2] + [to_peer(h2, k) for k in range(1, nd)]
            blocks = {}
            for batch in batches:
                for k, value in zip(batch, mlp_forward([hs[k] for k in batch], wg, wu, wd, batch == [0])):
                    blocks[k] = value
            gates, ups, acts = ([blocks[k][i] for k in range(nd)] for i in range(3))
            parts = [mid, blocks[0][3]] + [to_peer(blocks[k][3], k) for k in range(1, nd)]
            saved.append((stream, h, kv_all, qs, head_out, inv, low, mid, hs, gates, ups, acts))
            if layer + 1 < layers:
                attn.append(use_attention(pending))
        output = parts[0]
        for part in parts[1:]:
            output = output + part.astype(F32)

        def spread(keep, send):
            both = keep.astype(F32) + to_core(send).astype(F32)
            slabs = both.astype(BF16)
            total = both[0]
            for k in range(1, nz):
                total = total + to_z(slabs[k], k).astype(F32)
            return total.astype(BF16)

        def reduce_attention(keep, send):
            both = keep.astype(F32) + to_core(send).astype(F32)
            slabs = both.astype(BF16)
            total = both[0]
            for k in range(1, nd):
                total = total + to_peer(slabs[k], k).astype(F32)
            slabs = total.astype(BF16)
            mine = total[0]
            for k in range(1, nz):
                mine = mine + to_z(slabs[k], k).astype(F32)
            return mine

        grad, g_low = cotangent, cotangent.astype(BF16)
        results = []
        for layer in reversed(range(layers)):
            stream, h, kv_all, qs, head_out, inv, low, mid, hs, gates, ups, acts = saved[layer]
            wq, wkv, wo, gain_a, gain_m = attn[layer]
            wg, wu, wd = mlp[layer]
            gs = [g_low] + [to_peer(g_low, k) for k in range(1, nd)]
            blocks = {}
            for batch in batches:
                pick = lambda v: [v[k] for k in batch]
                for k, value in zip(batch, mlp_backward(pick(gs), pick(gates), pick(ups), wg, wu, wd, batch == [0])):
                    blocks[k] = value
            ggs, gus = ([blocks[k][i] for k in range(nd)] for i in range(2))
            parts = [blocks[0][2]] + [to_peer(blocks[k][2], k) for k in range(1, nd)]
            keep, send, dkeep, dsend = mlp_weight_grads(place, gs, acts, ggs, gus, hs, nz)
            parts, keep, send, dkeep, dsend = lax.optimization_barrier((parts, keep, send, dkeep, dsend))
            dgu, dwd = spread(keep, send), spread(dkeep, dsend)
            gmid, ga, ggain_m, gq, keep, send = attention_backward(
                bounds, grad, parts, mid, gain_m, wo, qs, kv_all, head_out, inv, cosine, sine, *lanes
            )
            both = (keep.astype(F32) + to_core(send).astype(F32)).astype(BF16)
            gkvs = [both[0]] + [to_z(both[k], k) for k in range(1, nz)]
            keep, send = attention_weight_grads(place, [(gq, h), (ga, low)], None, nd, nz, [[qc], [qc]])
            gkvs, keep, send = lax.optimization_barrier((gkvs, keep, send))
            first = reduce_attention(keep, send)
            grad, g_low, gkv_low, ggain_a = hidden_backward(gmid, stream, gain_a, gkvs, gq, wq, wkv, cosine, sine)
            gains = jnp.concatenate([ggain_a.reshape(nf, 1, qc), ggain_m.reshape(nf, 1, qc)], axis=2)
            gains = jnp.pad(gains, ((0, 0), (0, 7), (0, 0))).astype(BF16)
            keep, send = attention_weight_grads(place, [(gkv_low, h)], gains, nd, nz, [[kc, kc]])
            second = reduce_attention(keep, send)

            back = jnp.concatenate(
                [
                    dgu.reshape(2, sub, nd, rows).transpose(2, 0, 1, 3),
                    dwd.reshape(qc, nd, per, sub).transpose(1, 3, 2, 0).reshape(nd, 1, sub, per * qc),
                ],
                axis=1,
            )
            back = lax.all_to_all(back, "dp", 0, 0, tiled=True)
            results.append(
                (
                    second[2 * sizes[1], :qc],
                    first[:qc].T,
                    second[:kc].T,
                    second[sizes[1] : sizes[1] + kc].T,
                    first[sizes[0] : sizes[0] + qc].T,
                    second[2 * sizes[1], qc:],
                    back[:, 0].reshape(fc, rows).T.astype(F32),
                    back[:, 1].reshape(fc, rows).T.astype(F32),
                    back[:, 2].reshape(nd, sub, per, qc).transpose(2, 0, 1, 3).reshape(per * nd * sub, qc).astype(F32),
                )
            )
        results = results[::-1]
        return (output, grad) + tuple(jnp.stack([entry[n] for entry in results]) for n in range(9))

    return on_device


def solution(mesh):
    nd, nf = mesh.shape["dp"], mesh.shape["fsdp"]
    inner = Mesh(mesh.devices.reshape(nd, nf // 2, 2), ("dp", "zz", "core"))
    fs = ("zz", "core")
    rows = P(("dp", "zz", "core"), None)
    vector = P(None, fs)
    matrix = P(None, "dp", fs)
    in_specs = (rows, P(("dp", "zz", "core")), vector, matrix, matrix, matrix, matrix, vector, matrix, matrix, matrix, rows)
    out_specs = (rows, rows, vector, matrix, matrix, matrix, matrix, vector, matrix, matrix, matrix)
    return jax.shard_map(make(mesh), mesh=inner, in_specs=in_specs, out_specs=out_specs, check_vma=False)
```
